32 devices in a mesh: los: 8 (over z, x), sky: 4 (over y, core).
Axes of the slice: x: 2, y: 2, z: 4, core: 2. Of those that a mesh axis runs over, the one named last changes fastest.
Arguments:
- potentials: bfloat16 [32, 64, 4096], P('los', 'sky'), may hold values from -6 to 6
- shell_weight: float32 [32], P('los'), may hold values from 0.004 to 0.02
- shell_dist: float32 [32], P('los'), may hold values from 1 to 2.28, as said below
- source_dist: float32 [32], P('los'), may hold values from 1 to 2.28, as said below
Outputs:
- convergence: bfloat16 [32, 64, 4096], P('los', 'sky')
- shear_one: bfloat16 [32, 64, 4096], P('los', 'sky')
- shear_two: bfloat16 [32, 64, 4096], P('los', 'sky')
The draws below stay inside these ranges and needn't reach their ends.
Inputs may be any that keep to these rules, and one draw needn't show every extreme that they name: shell_dist rises strictly with the shell index. source_dist[s] lies strictly between shell_dist[s] and shell_dist[s + 1].
All inputs are finite; a program needn't handle non-finite values.
Results may differ from the reference program's by a relative error of at most 0.001.
Values may be sent and summed in bfloat16 or wider, within the bound.
A program may use at most 64 MiB of HBM per device.

```python
import math
import jax
import jax.numpy as jnp
from jax import lax

NCOLS = 4096
SHELLS = 32
NROWS = 64


def distances(key):
    steps = jax.random.uniform(jax.random.fold_in(key, 11), (SHELLS,), jnp.float32, 0.01, 0.04)
    shells = 1.0 + jnp.cumsum(steps) - steps
    gaps = jax.random.uniform(jax.random.fold_in(key, 12), (SHELLS,), jnp.float32, 0.3, 0.9) * steps
    return (shells, shells + gaps)


def draw_shell_dist(key, part):
    return distances(key)[0]


def draw_source_dist(key, part):
    return distances(key)[1]


def steps_of(rng, extent, cuts, low, high):
    def one(dim, blocks):
        draws = jax.random.uniform(jax.random.fold_in(jax.random.fold_in(rng, 6), dim), (blocks,), jnp.float32, low / len(cuts), high / len(cuts))
        return jnp.repeat(jnp.exp(draws), extent[dim] // blocks).reshape((-1,) + (1,) * (len(extent) - dim - 1))

    level = one(*cuts[0])
    for cut in cuts[1:]:
        level = level * one(*cut)
    return level


def gaussian(stream_key, dims, deviation, most, shards=(), kind=jnp.bfloat16):
    entries = jax.random.normal(stream_key, dims, jnp.float32) * deviation
    if len(shards) > 0:
        entries = steps_of(stream_key, dims, shards, -0.22, 0.18) * entries
    return jnp.clip(entries, min=-most, max=most).astype(kind)


def setup_inputs(seed: int = 0) -> dict:
    streams_of = jax.random.split(jax.random.key(seed), 5)
    potentials = gaussian(streams_of[0], (SHELLS, NROWS, NCOLS), 1.0, 6.0, ((0, 8), (1, 4)))
    shell_weight = jnp.clip(jnp.exp(math.log(0.02) - 1.6094378 * jax.random.uniform(streams_of[1], (SHELLS,), jnp.float32) ** steps_of(streams_of[1], (SHELLS,), ((0, 8),), -0.2, 0.2)), 0.004, 0.02)
    shell_dist = draw_shell_dist(jax.random.fold_in(streams_of[4], 71), 0)
    source_dist = draw_source_dist(jax.random.fold_in(streams_of[4], 71), 0)
    return dict(potentials=potentials, shell_weight=shell_weight, shell_dist=shell_dist, source_dist=source_dist)


def first_diff(field, axis):
    return (jnp.roll(field, 2, axis=axis) - 8.0 * jnp.roll(field, 1, axis=axis) + 8.0 * jnp.roll(field, -1, axis=axis) - jnp.roll(field, -2, axis=axis)) / 12.0


def second_diff(field, axis):
    return (-jnp.roll(field, 2, axis=axis) + 16.0 * jnp.roll(field, 1, axis=axis) - 30.0 * field + 16.0 * jnp.roll(field, -1, axis=axis) - jnp.roll(field, -2, axis=axis)) / 12.0


def reference(potentials, shell_weight, shell_dist, source_dist):
    near_weight = shell_weight * shell_dist
    far_weight = near_weight * shell_dist
    start = jnp.zeros((potentials.shape[1], potentials.shape[2]), jnp.float32)

    def advance(carry, items):
        running_near, running_far = carry
        potential, near_one, far_one, source_one = items
        field = potential.astype(jnp.float32)
        running_near = running_near + near_one * field
        running_far = running_far + far_one * field
        lens_map = running_near - running_far / source_one
        second_x = second_diff(lens_map, 1)
        second_y = second_diff(lens_map, 0)
        cross = first_diff(first_diff(lens_map, 1), 0)
        convergence = (0.5 * (second_x + second_y)).astype(jnp.bfloat16)
        shear_one = (0.5 * (second_x - second_y)).astype(jnp.bfloat16)
        shear_two = cross.astype(jnp.bfloat16)
        return (running_near, running_far), (convergence, shear_one, shear_two)

    carry, outputs = lax.scan(advance, (start, start), (potentials, near_weight, far_weight, source_dist))
    return outputs[0], outputs[1], outputs[2]
```

```python
import functools

import jax
import jax.numpy as jnp
from jax import lax
from jax.experimental import pallas as pl
from jax.experimental.pallas import tpu as pltpu
from jax.sharding import PartitionSpec as P

MESH = pl.DeviceIdType.MESH
WIDTH = 128
TAIL = 6
EDGE_LAG = 6
BACK_LAG = 7


def schedule(n, tail, edge_lag, back_lag):
    mapped = {}
    for c in range(n):
        late = c < n - tail
        mapped[c] = c + (edge_lag if late else 0)
        mapped[n + c] = c + back_lag + (edge_lag if late else 0)
    span = 2 * n
    ready = {c: max(mapped[(c - 1) % span], mapped[c], mapped[(c + 1) % span]) for c in range(span)}
    steps = []
    for i in range(max(ready.values()) + 1):
        events = []
        if i < n:
            events.append(("sum", 0, i >= n - tail))
        if 0 <= i - back_lag < n:
            events.append(("take", n - back_lag, i - back_lag >= n - tail))
        for c in range(span):
            if mapped[c] == i:
                events.append(("lens", c - i, c % n >= n - tail))
        for c in range(span):
            if ready[c] == i:
                events.append(("out", c - i, False))
        steps.append(tuple(events))
    return steps


def lens_kernel(
    los, sky, n, tail, width, weight_hbm, dist_hbm, source_hbm, pot_hbm,
    conv_ref, one_ref, two_ref,
    weight_ref, dist_ref, source_ref, pot, edge_send, edge_recv, sent, own, got,
    onward, before, back, prefix, rim_send, rim_below, rim_above, rim_pot, lens, slopes,
    scalar_sem, load_sem, edge_ssem, edge_rsem, x_ssem, x_rsem, z_ssem, z_rsem, b_ssem, b_rsem,
    up_ssem, up_rsem, down_ssem, down_rsem,
):
    f32, bf16 = jnp.float32, jnp.bfloat16
    shells, rows = pot.shape[0], pot.shape[1]
    main, full, span = 2 * rows, 2 * rows + 8, 2 * n
    me = lax.axis_index("los")
    strip = lax.axis_index("sky")
    q = me // 2
    r = me % 2
    last = los // 2 - 1
    partner = me + 1 - 2 * r
    up = (strip + sky - 1) % sky
    down = (strip + 1) % sky
    mine_at = r * n
    theirs_at = (1 - r) * n

    scalars = [
        pltpu.make_async_copy(src, dst, scalar_sem.at[i])
        for i, (src, dst) in enumerate(
            ((weight_hbm, weight_ref), (dist_hbm, dist_ref), (source_hbm, source_ref))
        )
    ]
    for copy in scalars:
        copy.start()
    groups = load_sem.shape[0] // 2
    wide = n // groups * width
    loads = []
    for g in range(2 * groups):
        part = (1 - r) if g < groups else r
        cols = pl.ds(pl.multiple_of((part * groups + g % groups) * wide, 128), wide)
        loads.append(
            pltpu.make_async_copy(pot_hbm.at[:, :, cols], pot.at[:, :, cols], load_sem.at[g])
        )
        loads[-1].start()

    barrier = pltpu.get_barrier_semaphore()
    pl.semaphore_signal(barrier, inc=1, device_id={"los": partner}, device_id_type=MESH)
    pl.semaphore_signal(barrier, inc=1, device_id={"sky": up}, device_id_type=MESH)
    pl.semaphore_signal(barrier, inc=1, device_id={"sky": down}, device_id_type=MESH)

    @pl.when(q > 0)
    def _():
        pl.semaphore_signal(barrier, inc=1, device_id={"los": me - 2}, device_id_type=MESH)

    @pl.when(q < last)
    def _():
        pl.semaphore_signal(barrier, inc=1, device_id={"los": me + 2}, device_id_type=MESH)

    def columns(b):
        return pl.ds(pl.multiple_of(b * width, 128), width)

    @pl.when(q == 0)
    def _():
        def clear(c, carry):
            before[c] = jnp.zeros((full, width), f32)
            return carry

        lax.fori_loop(0, n, clear, 0)

    for copy in scalars:
        copy.wait()
    scale = 1.0 / 24.0
    near = [weight_ref[j] * dist_ref[j] * scale for j in range(shells)]
    far = [near[j] * dist_ref[j] for j in range(shells)]
    row = lax.broadcasted_iota(jnp.int32, (8, width), 0)
    lane = lax.broadcasted_iota(jnp.int32, (8, width), 1)
    inverse = [1.0 / jnp.full((8, width), source_ref[j], f32) for j in range(shells)]

    def tall(x):
        return jnp.concatenate([x] * (rows // 8), axis=0)

    def totals(b):
        total_near = jnp.zeros((rows, width), f32)
        total_far = jnp.zeros((rows, width), f32)
        for j in range(shells):
            block = pot[j, :, columns(b)].astype(f32)
            total_near = total_near + near[j] * block
            total_far = total_far + far[j] * block
        return total_near, total_far

    def remote(src, dst, ssem, rsem, **where):
        return pltpu.make_async_remote_copy(
            src_ref=src, dst_ref=dst, send_sem=ssem, recv_sem=rsem,
            device_id=where, device_id_type=MESH,
        )

    def part(ref, c, rim):
        return ref.at[c, pl.ds(0, full if rim else main)]

    def x_copy(c, rim):
        return remote(part(sent, c, rim), part(got, c, rim), x_ssem.at[c], x_rsem.at[c], los=partner)

    def z_copy(c, rim):
        return remote(
            part(onward, c, rim), part(before, c, rim), z_ssem.at[c], z_rsem.at[c], los=me + 2
        )

    def b_copy(c, rim):
        return remote(
            part(back, c, rim), part(prefix, mine_at + c, rim), b_ssem.at[c], b_rsem.at[c], los=partner
        )

    def b_arrival(c, rim):
        return remote(
            part(back, c, rim), part(prefix, theirs_at + c, rim), b_ssem.at[c], b_rsem.at[c], los=partner
        )

    def up_copy(b):
        return remote(rim_send.at[b], rim_below.at[b], up_ssem.at[b], up_rsem.at[b], sky=up)

    def down_copy(b):
        return remote(rim_send.at[b], rim_above.at[b], down_ssem.at[b], down_rsem.at[b], sky=down)

    edges = [
        remote(edge_send.at[0], edge_recv.at[0], edge_ssem.at[0], edge_rsem.at[0], sky=up),
        remote(edge_send.at[1], edge_recv.at[1], edge_ssem.at[1], edge_rsem.at[1], sky=down),
    ]

    def fill(ref, c, b):
        total_near, total_far = totals(b)
        ref[c, :rows] = total_near
        ref[c, rows:main] = total_far

    loads[0].wait()
    fill(sent, 0, theirs_at)

    peers = 3 + (q > 0).astype(jnp.int32) + (q < last).astype(jnp.int32)
    pl.semaphore_wait(barrier, peers)
    x_copy(0, n - tail <= 0).start()

    def send_totals(c, carry):
        fill(sent, c, theirs_at + c)
        x_copy(c, False).start()
        return carry

    early = min(n // groups, n - tail)
    lax.fori_loop(1, early, send_totals, 0)
    for copy in loads[1:]:
        copy.wait()

    def pack(b, carry):
        top = jnp.zeros((8, width), f32)
        bottom = jnp.zeros((8, width), f32)
        for j in range(shells):
            block = pot[j, :, columns(b)].astype(f32)
            mine = (row >= 2 * j) & (row < 2 * j + 2)
            top = jnp.where(mine, pltpu.roll(block[:8], (2 * j) % 8, 0), top)
            bottom = jnp.where(mine, pltpu.roll(block[rows - 8 :], (2 * j + 2) % 8, 0), bottom)
        edge_send[0, :, columns(b)] = top.astype(bf16)
        edge_send[1, :, columns(b)] = bottom.astype(bf16)
        return carry

    lax.fori_loop(0, span, pack, 0, unroll=4)
    for copy in edges:
        copy.start()
    lax.fori_loop(early, n - tail, send_totals, 0)

    def tail_totals(c, carry):
        fill(sent, c, theirs_at + c)
        return carry

    lax.fori_loop(n - tail, n, tail_totals, 0)

    def own_totals(c, carry):
        fill(own, c, mine_at + c)
        return carry

    lax.fori_loop(0, n, own_totals, 0, unroll=2)

    for copy in edges:
        copy.wait_recv()

    inner = (row >= 2) & (row < 6)

    def rims(b, total_of):
        below = edge_recv[0, :, columns(b)].astype(f32)
        above = edge_recv[1, :, columns(b)].astype(f32)
        total = jnp.zeros((8, width), f32)
        for j in range(shells):
            tile = jnp.where(
                row < 2,
                pltpu.roll(below, (8 - 2 * j) % 8, 0),
                jnp.where(
                    row < 4,
                    pltpu.roll(below, (10 - 2 * j) % 8, 0),
                    jnp.where(
                        row < 6,
                        pltpu.roll(above, (12 - 2 * j) % 8, 0),
                        pltpu.roll(above, (14 - 2 * j) % 8, 0),
                    ),
                ),
            )
            scaled = tile * jnp.where(inner, far[j], near[j])
            rim_pot[b, j] = scaled
            total = total + scaled
        if total_of is not None:
            ref, c = total_of
            ref[c, main:full] = total

    def tail_rims(c, carry):
        rims(theirs_at + c, (sent, c))
        x_copy(c, True).start()
        return carry

    def own_rims(c, carry):
        rims(mine_at + c, (own, c))
        return carry

    def other_rims(c, carry):
        rims(mine_at + c, None)
        rims(theirs_at + c, None)
        return carry

    lax.fori_loop(n - tail, n, tail_rims, 0)
    lax.fori_loop(n - tail, n, own_rims, 0)
    lax.fori_loop(0, n - tail, other_rims, 0)

    is_odd = r.astype(f32)
    is_even = 1.0 - is_odd

    def send_rim(b, sums):
        first_near, last_near = sums[:8], sums[rows - 8 : rows]
        first_far, last_far = sums[rows : rows + 8], sums[main - 8 : main]
        rim_send[b] = jnp.where(
            row < 2,
            first_near,
            jnp.where(
                row < 4,
                pltpu.roll(first_far, 2, 0),
                jnp.where(row < 6, pltpu.roll(last_far, 6, 0), last_near),
            ),
        )
        up_copy(b).start()
        down_copy(b).start()

    def add_up(c, rim):
        x_copy(c, rim).wait_recv()

        @pl.when(q > 0)
        def _():
            z_copy(c, rim).wait_recv()

        size = full if rim else main
        mine, other, base = own[c, :size], got[c, :size], before[c, :size]
        onward[c, :size] = base + (mine + other)

        @pl.when(q < last)
        def _():
            z_copy(c, rim).start()

        back[c, :size] = base + is_even * mine
        b_copy(c, rim).start()
        kept = base + is_odd * other
        prefix[mine_at + c, :size] = kept
        if not rim:
            send_rim(mine_at + c, kept)

    def take(c, rim):
        b_arrival(c, rim).wait_recv()
        if not rim:
            send_rim(theirs_at + c, prefix[theirs_at + c, :main])

    def map_block(b, rim):
        run_near = prefix[b, :rows]
        run_far = prefix[b, rows:main]
        if rim:
            edge = prefix[b, main:full]
        else:
            up_copy(b).wait_recv()
            down_copy(b).wait_recv()
            edge = jnp.where(row < 4, rim_below[b], rim_above[b])
        for j in range(shells):
            block = pot[j, :, columns(b)].astype(f32)
            run_near = run_near + near[j] * block
            run_far = run_far + far[j] * block
            edge = edge + rim_pot[b, j]
            far_edge = jnp.where(row < 4, pltpu.roll(edge, 6, 0), pltpu.roll(edge, 2, 0))
            border = edge - far_edge * inverse[j]
            lens[b, j, :8] = border
            lens[b, j, 8 : 8 + rows] = run_near - run_far * tall(inverse[j])
            lens[b, j, 8 + rows :] = border

    tile = 8 + rows

    def stack(x, count):
        return jnp.concatenate([x] * count, axis=0)

    lanes = stack(lane, tile // 8)

    def out_block(b):
        left_b = (b + span - 1) % span
        right_b = (b + 1) % span
        cols = columns(b)
        for j in range(shells):
            centre = lens[b, j, :tile]
            left = lens[left_b, j, :tile]
            right = lens[right_b, j, :tile]

            def shift(k):
                if k > 0:
                    joined = jnp.where(lanes >= width - k, left, centre)
                else:
                    joined = jnp.where(lanes < -k, right, centre)
                return pltpu.roll(joined, k % width, 1)

            left1, right1, left2, right2 = shift(1), shift(-1), shift(2), shift(-2)
            slope = (left2 - right2) + 8.0 * (right1 - left1)
            slopes[j, :tile] = slope
            slopes[j, tile:] = slope[:8]
            second_x = (16.0 * (left1 + right1) - (left2 + right2))[8:]

            def rows_at(ref, k):
                return ref[8 + k : 8 + k + rows]

            here = lens.at[b, j]
            second_y = 16.0 * (rows_at(here, -1) + rows_at(here, 1)) - (
                rows_at(here, -2) + rows_at(here, 2)
            )
            tilt = slopes.at[j]
            cross = (rows_at(tilt, -2) - rows_at(tilt, 2)) + 8.0 * (
                rows_at(tilt, 1) - rows_at(tilt, -1)
            )
            conv_ref[j, :, cols] = (second_x + second_y - 60.0 * centre[8:]).astype(bf16)
            one_ref[j, :, cols] = (second_x - second_y).astype(bf16)
            two_ref[j, :, cols] = (cross * (1.0 / 6.0)).astype(bf16)

    def block_at(c):
        half = (c >= n).astype(jnp.int32)
        return ((r + half) % 2) * n + c - half * n

    def run(edge_lag, back_lag):
        steps = schedule(n, tail, edge_lag, back_lag)
        start = 0
        while start < len(steps):
            stop = start + 1
            while stop < len(steps) and steps[stop] == steps[start]:
                stop += 1

            def body(i, carry, events=steps[start]):
                for event, offset, rim in events:
                    c = i + offset
                    if event == "sum":
                        add_up(c, rim)
                    elif event == "take":
                        take(c - n, rim)
                    elif event == "lens":
                        map_block(block_at(c), rim)
                    else:
                        out_block(block_at(c))
                return carry

            lax.fori_loop(start, stop, body, 0)
            start = stop

    @pl.when(q < 2)
    def _():
        run(EDGE_LAG, n)

    @pl.when(q >= 2)
    def _():
        run(EDGE_LAG, BACK_LAG)

    for copy in edges:
        copy.wait_send()

    def finish(rim):
        def body(c, carry):
            x_copy(c, rim).wait_send()
            b_copy(c, rim).wait_send()

            @pl.when(q < last)
            def _():
                z_copy(c, rim).wait_send()

            if not rim:
                for b in (c, n + c):
                    up_copy(b).wait_send()
                    down_copy(b).wait_send()
            return carry

        return body

    lax.fori_loop(0, n - tail, finish(False), 0)
    lax.fori_loop(n - tail, n, finish(True), 0)


def store_kernel(a, b, c, to_a, to_b, to_c, sems):
    copies = [
        pltpu.make_async_copy(src.at[j], dst.at[j], sems.at[m, j])
        for m, (src, dst) in enumerate(((a, to_a), (b, to_b), (c, to_c)))
        for j in range(a.shape[0])
    ]
    for copy in copies:
        copy.start()
    for copy in copies:
        copy.wait()


def on_device(los, sky, potentials, shell_weight, shell_dist, source_dist):
    shells, rows, ncols = potentials.shape
    width = WIDTH
    n = ncols // 2 // width
    tail = min(n, TAIL)
    groups = next(g for g in (4, 2, 1) if n % g == 0)
    f32, bf16 = jnp.float32, jnp.bfloat16
    dma = pltpu.SemaphoreType.DMA
    vmem = pl.BlockSpec(memory_space=pltpu.VMEM)
    anywhere = pl.BlockSpec(memory_space=pl.ANY)
    full = 2 * rows + 8
    message = pltpu.VMEM((n, full, width), f32)
    small = pltpu.VMEM((2 * n, 8, width), f32)
    scalar = pltpu.SMEM((shells,), f32)
    staged = pl.pallas_call(
        functools.partial(lens_kernel, los, sky, n, tail, width),
        out_shape=[pltpu.VMEM(potentials.shape, bf16)] * 3,
        in_specs=[anywhere] * 4,
        out_specs=[vmem] * 3,
        scratch_shapes=[
            scalar, scalar, scalar,
            pltpu.VMEM(potentials.shape, bf16),
            pltpu.VMEM((2, 8, ncols), bf16),
            pltpu.VMEM((2, 8, ncols), bf16),
            message, message, message, message, message, message,
            pltpu.VMEM((2 * n, full, width), f32),
            small, small, small,
            pltpu.VMEM((2 * n, shells, 8, width), f32),
            pltpu.VMEM((2 * n, shells, rows + 16, width), f32),
            pltpu.VMEM((shells, rows + 16, width), f32),
            dma((3,)), dma((2 * groups,)), dma((2,)), dma((2,)),
            dma((n,)), dma((n,)), dma((n,)), dma((n,)), dma((n,)), dma((n,)),
            dma((2 * n,)), dma((2 * n,)), dma((2 * n,)), dma((2 * n,)),
        ],
        compiler_params=pltpu.CompilerParams(collective_id=0, has_side_effects=True),
    )(shell_weight, shell_dist, source_dist, potentials)
    return tuple(pl.pallas_call(
        store_kernel,
        out_shape=[jax.ShapeDtypeStruct(potentials.shape, bf16)] * 3,
        in_specs=[vmem] * 3,
        out_specs=[anywhere] * 3,
        scratch_shapes=[dma((3, shells))],
    )(*[pltpu.with_memory_space_constraint(x, pltpu.VMEM) for x in staged]))


def solution(mesh):
    return jax.shard_map(
        functools.partial(on_device, mesh.shape["los"], mesh.shape["sky"]),
        mesh=mesh,
        in_specs=(P("los", "sky", None), P("los"), P("los"), P("los")),
        out_specs=(P("los", "sky", None), P("los", "sky", None), P("los", "sky", None)),
        check_vma=False,
    )
```

```python
import functools

import jax
import jax.numpy as jnp
from jax import lax
from jax.experimental import pallas as pl
from jax.experimental.pallas import tpu as pltpu
from jax.sharding import PartitionSpec as P

MESH = pl.DeviceIdType.MESH
WIDTH = 128
TAIL = 8
EDGE_LAG = 6
BACK_LAG = 7


def schedule(n, tail, edge_lag, back_lag):
    mapped = {}
    for c in range(n):
        late = c < n - tail
        mapped[c] = c + (edge_lag if late else 0)
        mapped[n + c] = c + back_lag + (edge_lag if late else 0)
    span = 2 * n
    ready = {c: max(mapped[(c - 1) % span], mapped[c], mapped[(c + 1) % span]) for c in range(span)}
    steps = []
    for i in range(max(ready.values()) + 1):
        events = []
        if i < n:
            events.append(("sum", 0, i >= n - tail))
        if 0 <= i - back_lag < n:
            events.append(("take", n - back_lag, i - back_lag >= n - tail))
        for c in range(span):
            if mapped[c] == i:
                events.append(("lens", c - i, c % n >= n - tail))
        for c in range(span):
            if ready[c] == i:
                events.append(("out", c - i, False))
        steps.append(tuple(events))
    return steps


def lens_kernel(
    los, sky, n, tail, width, weight_hbm, dist_hbm, source_hbm, pot_hbm,
    conv_ref, one_ref, two_ref,
    scalar_ref, pot, edge_send, edge_recv, sent, own, inbox,
    onward, back, prefix, rim_send, rim_recv, rim_pot, lens, slopes,
    scalar_sem, load_sem, edge_sems, send_sems, sum_rsem, b_rsem, rim_rsem,
):
    f32, bf16 = jnp.float32, jnp.bfloat16
    shells, rows = pot.shape[0], pot.shape[1]
    main, full, span = 2 * rows, 2 * rows + 8, 2 * n
    me = lax.axis_index("los")
    strip = lax.axis_index("sky")
    q = me // 2
    r = me % 2
    last = los // 2 - 1
    partner = me + 1 - 2 * r
    up = (strip + sky - 1) % sky
    down = (strip + 1) % sky
    mine_at = r * n
    theirs_at = (1 - r) * n

    for i, src in enumerate((weight_hbm, dist_hbm, source_hbm)):
        pltpu.make_async_copy(src, scalar_ref.at[i], scalar_sem.at[0]).start()
    first = max(1, n // 4)
    loads = []
    for g, (at, count) in enumerate(
        ((theirs_at, first), (theirs_at + first, n - first), (mine_at, n))
    ):
        if count > 0:
            cols = pl.ds(pl.multiple_of(at * width, 128), count * width)
            loads.append(
                pltpu.make_async_copy(pot_hbm.at[:, :, cols], pot.at[:, :, cols], load_sem.at[g])
            )
            loads[-1].start()

    barrier = pltpu.get_barrier_semaphore()
    pl.semaphore_signal(barrier, inc=1, device_id={"los": partner}, device_id_type=MESH)
    pl.semaphore_signal(barrier, inc=1, device_id={"sky": up}, device_id_type=MESH)
    pl.semaphore_signal(barrier, inc=1, device_id={"sky": down}, device_id_type=MESH)

    @pl.when(q > 0)
    def _():
        pl.semaphore_signal(barrier, inc=1, device_id={"los": me - 2}, device_id_type=MESH)

    @pl.when(q < last)
    def _():
        pl.semaphore_signal(barrier, inc=1, device_id={"los": me + 2}, device_id_type=MESH)

    def columns(b):
        return pl.ds(pl.multiple_of(b * width, 128), width)

    @pl.when(q == 0)
    def _():
        def clear(c, carry):
            base = pl.multiple_of(c * 8, 8)
            inbox[1, pl.ds(base, 8)] = jnp.zeros((8, width), f32)
            return carry

        lax.fori_loop(0, inbox.shape[1] // 8, clear, 0, unroll=8)

    pltpu.make_async_copy(scalar_ref, scalar_ref, scalar_sem.at[0]).wait()
    scale = 1.0 / 24.0
    near = [scalar_ref[0, j] * scalar_ref[1, j] * scale for j in range(shells)]
    far = [near[j] * scalar_ref[1, j] for j in range(shells)]
    row = lax.broadcasted_iota(jnp.int32, (8, width), 0)
    lane = lax.broadcasted_iota(jnp.int32, (8, width), 1)
    inverse = [1.0 / jnp.full((8, width), scalar_ref[2, j], f32) for j in range(shells)]

    def tall(x):
        return jnp.concatenate([x] * (rows // 8), axis=0)

    def totals(b):
        total_near = jnp.zeros((rows, width), f32)
        total_far = jnp.zeros((rows, width), f32)
        for j in range(shells):
            block = pot[j, :, columns(b)].astype(f32)
            total_near = total_near + near[j] * block
            total_far = total_far + far[j] * block
        return total_near, total_far

    def remote(src, dst, ssem, rsem, **where):
        return pltpu.make_async_remote_copy(
            src_ref=src, dst_ref=dst, send_sem=ssem, recv_sem=rsem,
            device_id=where, device_id_type=MESH,
        )

    def at(c, rim):
        start = c * main + ((c - (n - tail)) * 8 if rim else 0)
        return pl.ds(pl.multiple_of(start, 8), full if rim else main)

    def x_copy(c, rim):
        rows_of = at(c, rim)
        return remote(
            sent.at[rows_of], inbox.at[0, rows_of], send_sems.at[0], sum_rsem.at[c], los=partner
        )

    def z_copy(c, rim):
        rows_of = at(c, rim)
        return remote(
            onward.at[rows_of], inbox.at[1, rows_of], send_sems.at[1], sum_rsem.at[c], los=me + 2
        )

    def b_copy(c, rim):
        rows_of = at(c, rim)
        return remote(
            back.at[rows_of], prefix.at[r, rows_of], send_sems.at[2], b_rsem.at[c], los=partner
        )

    def arrived(ref, sem):
        pltpu.make_async_copy(ref, ref, sem).wait()

    def slot(b):
        return b - (b // n) * tail

    def rim_copies(b):
        src, dst, sem = rim_send.at[slot(b)], rim_recv.at[slot(b)], rim_rsem.at[slot(b)]
        return (
            remote(src, dst.at[0], send_sems.at[3], sem, sky=up),
            remote(src, dst.at[1], send_sems.at[3], sem, sky=down),
        )

    edges = [
        remote(edge_send.at[0], edge_recv.at[0], edge_sems.at[0], edge_sems.at[1], sky=up),
        remote(edge_send.at[1], edge_recv.at[1], edge_sems.at[0], edge_sems.at[1], sky=down),
    ]

    def fill(ref, c, b, rim=False):
        total_near, total_far = totals(b)
        start = at(c, rim).start
        ref[pl.ds(start, rows)] = total_near
        ref[pl.ds(start + rows, rows)] = total_far

    loads[0].wait()
    fill(sent, 0, theirs_at, n == tail)

    peers = 3 + (q > 0).astype(jnp.int32) + (q < last).astype(jnp.int32)
    pl.semaphore_wait(barrier, peers)
    if n > tail:
        x_copy(0, False).start()

    def send_totals(c, carry):
        fill(sent, c, theirs_at + c)
        x_copy(c, False).start()
        return carry

    early = min(first, n - tail)
    lax.fori_loop(1, early, send_totals, 0)
    for copy in loads[1:]:
        copy.wait()

    def pack(b, carry):
        top = jnp.zeros((8, width), f32)
        bottom = jnp.zeros((8, width), f32)
        for j in range(shells):
            block = pot[j, :, columns(b)].astype(f32)
            mine = (row >= 2 * j) & (row < 2 * j + 2)
            top = jnp.where(mine, pltpu.roll(block[:8], (2 * j) % 8, 0), top)
            bottom = jnp.where(mine, pltpu.roll(block[rows - 8 :], (2 * j + 2) % 8, 0), bottom)
        edge_send[0, :, columns(b)] = top.astype(bf16)
        edge_send[1, :, columns(b)] = bottom.astype(bf16)
        return carry

    lax.fori_loop(0, span, pack, 0, unroll=4)
    for copy in edges:
        copy.start()
    lax.fori_loop(max(1, early), n - tail, send_totals, 0)

    def tail_totals(c, carry):
        fill(sent, c, theirs_at + c, True)
        fill(own, c, mine_at + c, True)
        return carry

    lax.fori_loop(n - tail, n, tail_totals, 0)

    def own_totals(c, carry):
        fill(own, c, mine_at + c)
        return carry

    lax.fori_loop(0, n - tail, own_totals, 0)

    arrived(edge_recv, edge_sems.at[1])

    inner = (row >= 2) & (row < 6)

    def rims(b, total_of):
        below = edge_recv[0, :, columns(b)].astype(f32)
        above = edge_recv[1, :, columns(b)].astype(f32)
        total = jnp.zeros((8, width), f32)
        for j in range(shells):
            tile = jnp.where(
                row < 2,
                pltpu.roll(below, (8 - 2 * j) % 8, 0),
                jnp.where(
                    row < 4,
                    pltpu.roll(below, (10 - 2 * j) % 8, 0),
                    jnp.where(
                        row < 6,
                        pltpu.roll(above, (12 - 2 * j) % 8, 0),
                        pltpu.roll(above, (14 - 2 * j) % 8, 0),
                    ),
                ),
            )
            scaled = tile * jnp.where(inner, far[j], near[j])
            rim_pot[b, j] = scaled
            total = total + scaled
        if total_of is not None:
            ref, c = total_of
            ref[pl.ds(at(c, True).start + main, 8)] = total

    def tail_rims(c, carry):
        rims(theirs_at + c, (sent, c))
        x_copy(c, True).start()
        return carry

    def own_rims(c, carry):
        rims(mine_at + c, (own, c))
        return carry

    def other_rims(c, carry):
        rims(mine_at + c, None)
        rims(theirs_at + c, None)
        return carry

    lax.fori_loop(n - tail, n, tail_rims, 0)
    lax.fori_loop(n - tail, n, own_rims, 0)
    lax.fori_loop(0, n - tail, other_rims, 0)

    is_odd = r.astype(f32)
    is_even = 1.0 - is_odd

    def send_rim(b, sums):
        first_near, last_near = sums[:8], sums[rows - 8 : rows]
        first_far, last_far = sums[rows : rows + 8], sums[main - 8 : main]
        rim_send[slot(b)] = jnp.where(
            row < 2,
            first_near,
            jnp.where(
                row < 4,
                pltpu.roll(first_far, 2, 0),
                jnp.where(row < 6, pltpu.roll(last_far, 6, 0), last_near),
            ),
        )
        for copy in rim_copies(b):
            copy.start()

    def add_up(c, rim):
        rows_of = at(c, rim)

        @pl.when(q == 0)
        def _():
            arrived(inbox.at[0, rows_of], sum_rsem.at[c])

        @pl.when(q > 0)
        def _():
            arrived(inbox.at[:, rows_of], sum_rsem.at[c])

        mine, other, base = own[rows_of], inbox[0, rows_of], inbox[1, rows_of]
        onward[rows_of] = base + (mine + other)

        @pl.when(q < last)
        def _():
            z_copy(c, rim).start()

        back[rows_of] = base + is_even * mine
        b_copy(c, rim).start()
        kept = base + is_odd * other
        prefix[r, rows_of] = kept
        if not rim:
            send_rim(mine_at + c, kept)

    def take(c, rim):
        rows_of = at(c, rim)
        arrived(prefix.at[1 - r, rows_of], b_rsem.at[c])
        if not rim:
            send_rim(theirs_at + c, prefix[1 - r, rows_of])

    def map_block(b, rim):
        half = b // n
        c = b - half * n
        sums = prefix[half, at(c, rim)]
        run_near = sums[:rows]
        run_far = sums[rows:main]
        if rim:
            edge = sums[main:]
        else:
            arrived(rim_recv.at[slot(b)], rim_rsem.at[slot(b)])
            edge = jnp.where(row < 4, rim_recv[slot(b), 0], rim_recv[slot(b), 1])
        for j in range(shells):
            block = pot[j, :, columns(b)].astype(f32)
            run_near = run_near + near[j] * block
            run_far = run_far + far[j] * block
            edge = edge + rim_pot[b, j]
            far_edge = jnp.where(row < 4, pltpu.roll(edge, 6, 0), pltpu.roll(edge, 2, 0))
            border = edge - far_edge * inverse[j]
            lens[b, j, :8] = border
            lens[b, j, 8 : 8 + rows] = run_near - run_far * tall(inverse[j])
            lens[b, j, 8 + rows :] = border

    tile = 8 + rows

    def stack(x, count):
        return jnp.concatenate([x] * count, axis=0)

    lanes = stack(lane, tile // 8)

    def out_block(b):
        left_b = (b + span - 1) % span
        right_b = (b + 1) % span
        cols = columns(b)
        for j in range(shells):
            centre = lens[b, j, :tile]
            left = lens[left_b, j, :tile]
            right = lens[right_b, j, :tile]

            def shift(k):
                if k > 0:
                    joined = jnp.where(lanes >= width - k, left, centre)
                else:
                    joined = jnp.where(lanes < -k, right, centre)
                return pltpu.roll(joined, k % width, 1)

            left1, right1, left2, right2 = shift(1), shift(-1), shift(2), shift(-2)
            slope = (left2 - right2) + 8.0 * (right1 - left1)
            slopes[j, :tile] = slope
            slopes[j, tile:] = slope[:8]
            second_x = (16.0 * (left1 + right1) - (left2 + right2))[8:]

            def rows_at(ref, k):
                return ref[8 + k : 8 + k + rows]

            here = lens.at[b, j]
            second_y = 16.0 * (rows_at(here, -1) + rows_at(here, 1)) - (
                rows_at(here, -2) + rows_at(here, 2)
            )
            tilt = slopes.at[j]
            cross = (rows_at(tilt, -2) - rows_at(tilt, 2)) + 8.0 * (
                rows_at(tilt, 1) - rows_at(tilt, -1)
            )
            conv_ref[j, :, cols] = (second_x + second_y - 60.0 * centre[8:]).astype(bf16)
            one_ref[j, :, cols] = (second_x - second_y).astype(bf16)
            two_ref[j, :, cols] = (cross * (1.0 / 6.0)).astype(bf16)

    def block_at(c):
        half = (c >= n).astype(jnp.int32)
        return ((r + half) % 2) * n + c - half * n

    def run(edge_lag, back_lag):
        steps = schedule(n, tail, edge_lag, back_lag)
        start = 0
        while start < len(steps):
            stop = start + 1
            while stop < len(steps) and steps[stop] == steps[start]:
                stop += 1

            def body(i, carry, events=steps[start]):
                for event, offset, rim in events:
                    c = i + offset
                    if event == "sum":
                        add_up(c, rim)
                    elif event == "take":
                        take(c - n, rim)
                    elif event == "lens":
                        map_block(block_at(c), rim)
                    else:
                        out_block(block_at(c))
                return carry

            lax.fori_loop(start, stop, body, 0)
            start = stop

    @pl.when(q < 2)
    def _():
        run(EDGE_LAG, n)

    @pl.when(q >= 2)
    def _():
        run(EDGE_LAG, BACK_LAG)

    arrived(edge_send, edge_sems.at[0])
    arrived(sent, send_sems.at[0])
    arrived(back, send_sems.at[2])
    if n > tail:
        arrived(rim_recv, send_sems.at[3])

    @pl.when(q < last)
    def _():
        arrived(onward, send_sems.at[1])


def store_kernel(a, b, c, to_a, to_b, to_c, sems):
    copies = [
        pltpu.make_async_copy(src.at[j], dst.at[j], sems.at[m, j])
        for m, (src, dst) in enumerate(((a, to_a), (b, to_b), (c, to_c)))
        for j in range(a.shape[0])
    ]
    for copy in copies:
        copy.start()
    for copy in copies:
        copy.wait()


def on_device(los, sky, potentials, shell_weight, shell_dist, source_dist):
    shells, rows, ncols = potentials.shape
    width = WIDTH
    n = ncols // 2 // width
    tail = min(n, TAIL)
    f32, bf16 = jnp.float32, jnp.bfloat16
    dma = pltpu.SemaphoreType.DMA
    vmem = pl.BlockSpec(memory_space=pltpu.VMEM)
    anywhere = pl.BlockSpec(memory_space=pl.ANY)
    lines = n * 2 * rows + tail * 8
    message = pltpu.VMEM((lines, width), f32)
    pair = pltpu.VMEM((2, lines, width), f32)
    slots = max(1, 2 * (n - tail))
    staged = pl.pallas_call(
        functools.partial(lens_kernel, los, sky, n, tail, width),
        out_shape=[pltpu.VMEM(potentials.shape, bf16)] * 3,
        in_specs=[anywhere] * 4,
        out_specs=[vmem] * 3,
        scratch_shapes=[
            pltpu.SMEM((3, shells), f32),
            pltpu.VMEM(potentials.shape, bf16),
            pltpu.VMEM((2, 8, ncols), bf16),
            pltpu.VMEM((2, 8, ncols), bf16),
            message, message, pair, message, message, pair,
            pltpu.VMEM((slots, 8, width), f32),
            pltpu.VMEM((slots, 2, 8, width), f32),
            pltpu.VMEM((2 * n, shells, 8, width), f32),
            pltpu.VMEM((2 * n, shells, rows + 16, width), f32),
            pltpu.VMEM((shells, rows + 16, width), f32),
            dma((1,)), dma((3,)), dma((2,)), dma((4,)), dma((n,)), dma((n,)), dma((slots,)),
        ],
        compiler_params=pltpu.CompilerParams(collective_id=0, has_side_effects=True),
    )(shell_weight, shell_dist, source_dist, potentials)
    return tuple(pl.pallas_call(
        store_kernel,
        out_shape=[jax.ShapeDtypeStruct(potentials.shape, bf16)] * 3,
        in_specs=[vmem] * 3,
        out_specs=[anywhere] * 3,
        scratch_shapes=[dma((3, shells))],
    )(*[pltpu.with_memory_space_constraint(x, pltpu.VMEM) for x in staged]))


def solution(mesh):
    return jax.shard_map(
        functools.partial(on_device, mesh.shape["los"], mesh.shape["sky"]),
        mesh=mesh,
        in_specs=(P("los", "sky", None), P("los"), P("los"), P("los")),
        out_specs=(P("los", "sky", None), P("los", "sky", None), P("los", "sky", None)),
        check_vma=False,
    )
```
